32 devices in a mesh: pb: 4 (over y, core), wa: 8 (over z, x).
Axes of the slice: x: 2, y: 2, z: 4, core: 2. Of those that a mesh axis runs over, the one named last changes fastest.
Arguments:
- state: float32 [2, 8388608], P(None, ('pb', 'wa')), may hold values from -6 to 6
- gate_bank: float32 [4, 2, 128, 128], replicated, may hold values from -0.375 to 0.375
- pass_order: int32 [4], replicated, may hold values from 0 to 3, each once
Outputs:
- evolved: float32 [2, 8388608], P(None, ('pb', 'wa'))
The draws below stay inside these ranges and needn't reach their ends.
Inputs may be any that keep to these rules, and one draw needn't show every extreme that they name: `pass_order`: each pass index 0 to 3 appears once.
All inputs are finite; a program needn't handle non-finite values.
Results may differ from the reference program's by a relative error of at most 0.0001.
Values sent between devices are 32-bit elements; how exact they have to be, the bound alone decides.
A program may use at most 64 MiB of HBM per device.

```python
import jax
import jax.numpy as jnp
from jax import lax

LQ = 18
GATE = 128
LAYERS = 2
PASSES = 4
AMPS = 8388608
N_PB = 4
N_WA = 8


def shard_levels(stream_key, dims, pieces, low, high):
    level = 1.0
    for axis_at, shards_of in pieces:
        draws = jax.random.uniform(jax.random.fold_in(jax.random.fold_in(stream_key, 6), axis_at), (shards_of,), jnp.float32, low / len(pieces), high / len(pieces))
        level = level * jnp.repeat(jnp.exp(draws), dims[axis_at] // shards_of).reshape((-1,) + (1,) * (len(dims) - 1 - axis_at))
    return level


def scatter_about(stream_key, dims, spread, bound, cuts=(), dtype=jnp.bfloat16):
    entries = spread * jax.random.normal(stream_key, dims, jnp.float32)
    if cuts:
        entries = entries * shard_levels(stream_key, dims, cuts, -0.22, 0.18)
    return jnp.clip(entries, -bound, bound).astype(dtype)


def setup_inputs(seed: int = 0) -> dict:
    arg_keys = jax.random.split(jax.random.key(seed), 4)
    return {
        "state": scatter_about(arg_keys[0], (2, AMPS), 1.0, 6.0, ((1, 32),), jnp.float32),
        "gate_bank": scatter_about(arg_keys[1], (PASSES, 2, GATE, GATE), (2 * GATE) ** -0.5, 0.375, (), jnp.float32),
        "pass_order": jax.random.permutation(arg_keys[2], PASSES).astype(jnp.int32),
    }


HIGH = lax.Precision.HIGHEST


def mix_left(gate, values):
    real = jnp.dot(gate[0], values[0], precision=HIGH) - jnp.dot(gate[1], values[1], precision=HIGH)
    imag = jnp.dot(gate[0], values[1], precision=HIGH) + jnp.dot(gate[1], values[0], precision=HIGH)
    return jnp.stack([real, imag])


def mix_right(gate, values):
    real = jnp.dot(values[0], gate[0].T, precision=HIGH) - jnp.dot(values[1], gate[1].T, precision=HIGH)
    imag = jnp.dot(values[1], gate[0].T, precision=HIGH) + jnp.dot(values[0], gate[1].T, precision=HIGH)
    return jnp.stack([real, imag])


def reference(state, gate_bank, pass_order):
    wa_bits = N_WA.bit_length() - 1
    middle = GATE // (2 * N_PB)
    rest = 2 ** LQ // GATE
    psi = state.astype(jnp.float32)
    for layer in range(LAYERS):
        first = gate_bank[pass_order[2 * layer]]
        psi = mix_right(first, psi.reshape(2, -1, GATE)).reshape(2, -1)
        second = gate_bank[pass_order[2 * layer + 1]]
        bit_pos = wa_bits - 1 if layer == 0 else 0
        low_wa = 2 ** bit_pos
        high_wa = N_WA // (2 * low_wa)
        shaped = psi.reshape(2, N_PB, high_wa, 2, low_wa, N_PB, 2, middle, rest)
        moved = jnp.transpose(shaped, (0, 1, 3, 7, 2, 4, 5, 6, 8))
        moved_shape = moved.shape
        mixed = mix_left(second, moved.reshape(2, GATE, -1)).reshape(moved_shape)
        psi = jnp.transpose(mixed, (0, 1, 4, 2, 5, 6, 7, 3, 8)).reshape(2, -1)
    return psi
```

```python
import functools

import jax
import jax.numpy as jnp
from jax import lax
from jax.experimental import pallas as pl
from jax.experimental.pallas import tpu as pltpu
from jax.sharding import PartitionSpec as P

MESH = pl.DeviceIdType.MESH
HIGH = lax.Precision.HIGHEST


def dot(a, b, contract=((1,), (0,)), precision=HIGH):
    return lax.dot_general(
        a, b, (contract, ((), ())), precision=precision, preferred_element_type=jnp.float32
    )


def dot_t(a, b):
    return dot(a, b, ((1,), (1,)))


def embed(real, imag):
    upper = jnp.concatenate([real, -imag], axis=1)
    lower = jnp.concatenate([imag, real], axis=1)
    return jnp.concatenate([upper, lower], axis=0)


def split(values):
    high = values.astype(jnp.bfloat16)
    return high, (values - high.astype(jnp.float32)).astype(jnp.bfloat16)


def dot3(a, b):
    def term(i, j):
        return dot(a[i], b[j], precision=None)

    return term(0, 0) + (term(0, 1) + term(1, 0))


def spread_rows(groups, mid, gate_rows, high):
    slot = lax.broadcasted_iota(jnp.int32, (2 * gate_rows, gate_rows), 0)
    row = lax.broadcasted_iota(jnp.int32, (2 * gate_rows, gate_rows), 1)
    a = row // (2 * mid)
    w0 = (row // mid) % 2
    m = row % mid
    return jnp.where(slot == ((w0 * groups + a) * 2 + high) * mid + m, 1.0, 0.0).astype(jnp.float32)


def kernel(groups, wa_count, mid, sub, order_hbm, bank_hbm, x_ref, out_ref, order_ref, bank_ref,
           lanes_gate, rows_gate, buf, obuf, landed, stage, zfs, zfr, zbs, zbr, fs, fr, bs, br,
           own, load, entered, round_sem, go):
    gate_rows = bank_ref.shape[2]
    rows = 2 * gate_rows
    halves = groups // 2
    a = lax.axis_index("pb")
    w = lax.axis_index("wa")
    half = wa_count // 2
    w2 = w // half
    w0 = w % 2
    wm = w - w2 * half - w0
    other = 1 - w2
    h = a // 2
    k = a % 2
    me = (a, w2, w0)

    def device(p):
        return (p[0], p[1] * half + wm + p[2])

    def slot(p):
        return (p[2] * groups + p[0]) * 2 + p[1]

    def held(ref, p):
        return ref.at[pl.ds(slot(p) * mid, mid)]

    def piece(ref, p):
        return ref.at[p[0] * 2 + p[1], :, p[2]]

    beside = [((a + da) % groups, w2, (w0 + dw0) % 2)
              for da in range(groups) for dw0 in range(2)][1:]
    plane = [((h + dh) % halves, (w0 + dw0) % 2) for dh in range(halves) for dw0 in range(2)]
    across = (a, other, w0)

    def remote(src, dst, send, recv, p):
        return pltpu.make_async_remote_copy(
            src_ref=src, dst_ref=dst, send_sem=send, recv_sem=recv,
            device_id=device(p), device_id_type=MESH)

    def cross(kd, hd, ks):
        return remote(x_ref.at[(hd * 2 + kd) * 2 + other], landed.at[ks, hd],
                      zfs.at[kd, hd], zfr.at[ks, hd], (h * 2 + kd, other, w0))

    def forward(p, src):
        return remote(piece(x_ref, p), held(buf, src), fs.at[slot(p)], fr.at[slot(src)], p)

    def relay(hd, xd, ks, src_h, src_x):
        src = (src_h * 2 + ks, other, src_x)
        return remote(landed.at[ks, hd, :, xd], held(buf, src),
                      fs.at[slot((hd * 2 + ks, other, xd))], fr.at[slot(src)],
                      (hd * 2 + k, w2, xd))

    def back(p, src):
        return remote(held(obuf, p), piece(out_ref, src), bs.at[slot(p)], br.at[slot(src)], p)

    def gather(hd, xd, kd, src_h, src_x):
        dst = (hd * 2 + kd, other, xd)
        return remote(held(obuf, dst), stage.at[kd, src_h, :, src_x],
                      bs.at[slot(dst)], br.at[slot((src_h * 2 + kd, other, src_x))],
                      (hd * 2 + k, w2, xd))

    def home(kd, hs, ks, side):
        return remote(stage.at[kd, hs], out_ref.at[(hs * 2 + ks) * 2 + side],
                      zbs.at[kd, hs], zbr.at[ks, hs], (h * 2 + kd, other, w0))

    def signal(sem, p):
        pl.semaphore_signal(sem, inc=1, device_id=device(p), device_id_type=MESH)

    barrier = pltpu.get_barrier_semaphore()

    @pl.when(w2 == 0)
    def _():
        signal(barrier, across)
        for p in beside:
            signal(barrier, p)

    @pl.when(w2 == 1)
    def _():
        pl.semaphore_wait(barrier, 1)
        signal(entered, across)
        for hd in range(halves):
            cross(k, hd, k).start()
        pl.semaphore_wait(go, 1)

    @pl.when(w2 == 0)
    def _():
        pl.semaphore_wait(entered, 1)
        for hd in range(halves):
            cross(k, hd, k).start()
        pl.semaphore_wait(barrier, len(beside))
        for p in beside:
            signal(round_sem, p)
        pl.semaphore_wait(round_sem, len(beside))
        signal(go, across)

    for hd in range(halves):
        cross(1 - k, hd, k).start()
    for p in beside:
        forward(p, me).start()
    fetch = [pltpu.make_async_copy(order_hbm, order_ref, load.at[0]),
             pltpu.make_async_copy(bank_hbm, bank_ref, load.at[1])]
    stay = pltpu.make_async_copy(piece(x_ref, me), held(buf, me), own.at[0])
    for copy in fetch + [stay]:
        copy.start()
    for copy in fetch:
        copy.wait()

    gates = [bank_ref[order_ref[j]] for j in range(4)]
    first = embed(gates[0][0], gates[0][1])
    third = embed(gates[2][0], gates[2][1])
    for i, part in enumerate(split(dot(first, third, ((0,), (1,))))):
        lanes_gate[i] = part
    real, imag = 0.0, 0.0
    for high in range(2):
        spread = spread_rows(groups, mid, gate_rows, high)
        real += dot_t(dot(spread, gates[3][0]), spread)
        imag += dot_t(dot(spread, gates[3][1]), spread)
    zero = jnp.zeros((gate_rows, gate_rows), jnp.float32)
    parts = []
    for part in range(2):
        g = gates[1][part]
        parts.append(jnp.concatenate([
            jnp.concatenate([g, zero], axis=1), jnp.concatenate([zero, g], axis=1)], axis=0))
    for i, part in enumerate(split(dot(embed(real, imag), jnp.concatenate(parts, axis=0)))):
        rows_gate[i] = part

    keep = []
    for flip in range(2):
        ks = k if flip == 0 else 1 - k
        for hd in range(halves):
            cross(ks, hd, ks).wait_recv()
        for dest in plane[1:]:
            relay(*dest, ks, h, w0).start()
        keep.append(pltpu.make_async_copy(
            landed.at[ks, h, :, w0], held(buf, (h * 2 + ks, other, w0)), own.at[1 + flip]))
        keep[-1].start()

    for p in beside:
        forward(p, p).wait_recv()
    for flip in range(2):
        ks = k if flip == 0 else 1 - k
        for src in plane[1:]:
            relay(*src, ks, *src).wait_recv()
    for copy in [stay] + keep:
        copy.wait()

    flat_in = buf.reshape(rows * sub, buf.shape[-1])
    flat_out = obuf.reshape(rows * sub, buf.shape[-1])
    for q in range(sub // 2):
        re = flat_in[pl.ds(2 * q, rows, sub), :]
        im = flat_in[pl.ds(2 * q + 1, rows, sub), :]
        mixed = dot3(split(jnp.concatenate([re, im], axis=1)), lanes_gate)
        done = dot3(rows_gate, split(mixed))
        flat_out[pl.ds(2 * q, rows, sub), :] = done[:rows, :gate_rows] - done[rows:, gate_rows:]
        flat_out[pl.ds(2 * q + 1, rows, sub), :] = done[:rows, gate_rows:] + done[rows:, :gate_rows]

    local = []
    for kd in range(2):
        for dest in plane[1:]:
            gather(*dest, kd, h, w0).start()
        local.append(pltpu.make_async_copy(
            held(obuf, (h * 2 + kd, other, w0)), stage.at[kd, h, :, w0], own.at[1 + kd]))
        local[-1].start()
    for p in beside:
        back(p, me).start()
    stay = pltpu.make_async_copy(held(obuf, me), piece(out_ref, me), own.at[0])
    stay.start()

    for kd in range(2):
        for src in plane[1:]:
            gather(*src, kd, *src).wait_recv()
        local[kd].wait()
        for hs in range(halves):
            home(kd, hs, k, w2).start()

    for p in beside:
        back(p, p).wait_recv()
    stay.wait()
    for ks in range(2):
        for hs in range(halves):
            home(ks, hs, ks, other).wait_recv()
    for kd in range(2):
        for hd in range(halves):
            cross(kd, hd, k).wait_send()
            home(kd, hd, k, w2).wait_send()
        for dest in plane[1:]:
            relay(*dest, kd, h, w0).wait_send()
            gather(*dest, kd, h, w0).wait_send()
    for p in beside:
        forward(p, me).wait_send()
        back(p, me).wait_send()


def per_device(groups, wa_count, state, gate_bank, pass_order):
    lanes = gate_bank.shape[2]
    mid = lanes // (2 * groups)
    size = state.shape[1]
    sub = 2 * size // (lanes * 4 * groups * mid)
    shape = (2 * groups, mid, 2, sub, lanes)
    x = state.reshape(2, size // lanes, lanes).transpose(1, 0, 2).reshape(shape)
    slots = 4 * groups
    dma = pltpu.SemaphoreType.DMA
    out = pl.pallas_call(
        functools.partial(kernel, groups, wa_count, mid, sub),
        out_shape=pltpu.VMEM(shape, jnp.float32),
        in_specs=[pl.BlockSpec(memory_space=pl.ANY)] * 3,
        out_specs=pl.BlockSpec(memory_space=pltpu.VMEM),
        scratch_shapes=[
            pltpu.SMEM(pass_order.shape, jnp.int32),
            pltpu.VMEM(gate_bank.shape, jnp.float32),
            pltpu.VMEM((2, 2 * lanes, 2 * lanes), jnp.bfloat16),
            pltpu.VMEM((2, 4 * lanes, 2 * lanes), jnp.bfloat16),
            pltpu.VMEM((2 * lanes, sub, lanes), jnp.float32),
            pltpu.VMEM((2 * lanes, sub, lanes), jnp.float32),
            pltpu.VMEM((2, groups // 2, mid, 2, sub, lanes), jnp.float32),
            pltpu.VMEM((2, groups // 2, mid, 2, sub, lanes), jnp.float32),
            dma((2, groups // 2)), dma((2, groups // 2)),
            dma((2, groups // 2)), dma((2, groups // 2)),
            dma((slots,)), dma((slots,)), dma((slots,)), dma((slots,)),
            dma((3,)), dma((2,)),
            pltpu.SemaphoreType.REGULAR, pltpu.SemaphoreType.REGULAR,
            pltpu.SemaphoreType.REGULAR,
        ],
        compiler_params=pltpu.CompilerParams(collective_id=0, has_side_effects=True),
    )(pass_order, gate_bank, x)
    return out.reshape(size // lanes, 2, lanes).transpose(1, 0, 2).reshape(2, size)


def solution(mesh):
    in_specs = (P(None, ("pb", "wa")), P(), P())
    out_specs = P(None, ("pb", "wa"))
    return jax.shard_map(
        functools.partial(per_device, mesh.shape["pb"], mesh.shape["wa"]),
        mesh=mesh, in_specs=in_specs, out_specs=out_specs, check_vma=False,
    )
```

```python
import functools

import jax
import jax.numpy as jnp
from jax import lax
from jax.experimental import pallas as pl
from jax.experimental.pallas import tpu as pltpu
from jax.sharding import PartitionSpec as P

MESH = pl.DeviceIdType.MESH
HIGH = lax.Precision.HIGHEST


def dot(a, b, contract=((1,), (0,)), precision=HIGH):
    return lax.dot_general(
        a, b, (contract, ((), ())), precision=precision, preferred_element_type=jnp.float32
    )


def dot_t(a, b):
    return dot(a, b, ((1,), (1,)))


def embed(real, imag):
    upper = jnp.concatenate([real, -imag], axis=1)
    lower = jnp.concatenate([imag, real], axis=1)
    return jnp.concatenate([upper, lower], axis=0)


def split(values):
    high = values.astype(jnp.bfloat16)
    return high, (values - high.astype(jnp.float32)).astype(jnp.bfloat16)


def dot3(a, b):
    def term(i, j):
        return dot(a[i], b[j], precision=None)

    return term(0, 0) + (term(0, 1) + term(1, 0))


def spread_rows(groups, mid, gate_rows, high):
    slot = lax.broadcasted_iota(jnp.int32, (2 * gate_rows, gate_rows), 0)
    row = lax.broadcasted_iota(jnp.int32, (2 * gate_rows, gate_rows), 1)
    a = row // (2 * mid)
    w0 = (row // mid) % 2
    m = row % mid
    return jnp.where(slot == ((w0 * groups + a) * 2 + high) * mid + m, 1.0, 0.0).astype(jnp.float32)


def kernel(groups, wa_count, mid, sub, order_hbm, bank_hbm, x_ref, out_ref, order_ref, bank_ref,
           lanes_gate, rows_gate, buf, obuf, landed, stage, zfs, zfr, zbs, zbr, fs, fr, bs, br,
           own, load, entered, round_sem, go):
    gate_rows = bank_ref.shape[2]
    rows = 2 * gate_rows
    halves = groups // 2
    a = lax.axis_index("pb")
    w = lax.axis_index("wa")
    half = wa_count // 2
    w2 = w // half
    w0 = w % 2
    wm = w - w2 * half - w0
    other = 1 - w2
    h = a // 2
    k = a % 2
    me = (a, w2, w0)

    def device(p):
        return (p[0], p[1] * half + wm + p[2])

    def slot(p):
        return (p[2] * groups + p[0]) * 2 + p[1]

    def held(ref, p):
        return ref.at[pl.ds(slot(p) * mid, mid)]

    def piece(ref, p):
        return ref.at[p[0] // 2, p[0] % 2, p[1], :, p[2]]

    beside = [((a + da) % groups, w2, (w0 + dw0) % 2)
              for da in range(groups) for dw0 in range(2)][1:]
    plane = [((h + dh) % halves, (w0 + dw0) % 2) for dh in range(halves) for dw0 in range(2)]
    across = (a, other, w0)

    def remote(src, dst, send, recv, p):
        return pltpu.make_async_remote_copy(
            src_ref=src, dst_ref=dst, send_sem=send, recv_sem=recv,
            device_id=device(p), device_id_type=MESH)

    def cross(kd, hd, ks):
        return remote(x_ref.at[hd, kd, other], landed.at[ks, hd],
                      zfs.at[kd, hd], zfr.at[ks, hd], (h * 2 + kd, other, w0))

    def forward(p, src):
        return remote(piece(x_ref, p), held(buf, src), fs.at[slot(p)], fr.at[slot(src)], p)

    def relay(hd, xd, ks, src_h, src_x):
        src = (src_h * 2 + ks, other, src_x)
        return remote(landed.at[ks, hd, :, xd], held(buf, src),
                      fs.at[slot((hd * 2 + ks, other, xd))], fr.at[slot(src)],
                      (hd * 2 + k, w2, xd))

    def back(p, src):
        return remote(held(obuf, p), piece(out_ref, src), bs.at[slot(p)], br.at[slot(src)], p)

    def gather(hd, xd, kd, src_h, src_x):
        dst = (hd * 2 + kd, other, xd)
        return remote(held(obuf, dst), stage.at[kd, src_h, :, src_x],
                      bs.at[slot(dst)], br.at[slot((src_h * 2 + kd, other, src_x))],
                      (hd * 2 + k, w2, xd))

    def home(kd, hs, ks, side):
        return remote(stage.at[kd, hs], out_ref.at[hs, ks, side],
                      zbs.at[kd, hs], zbr.at[ks, hs], (h * 2 + kd, other, w0))

    def signal(sem, p):
        pl.semaphore_signal(sem, inc=1, device_id=device(p), device_id_type=MESH)

    barrier = pltpu.get_barrier_semaphore()

    @pl.when(w2 == 0)
    def _():
        signal(barrier, across)
        for p in beside:
            signal(barrier, p)

    @pl.when(w2 == 1)
    def _():
        pl.semaphore_wait(barrier, 1)
        signal(entered, across)
        for hd in range(halves):
            cross(k, hd, k).start()
        pl.semaphore_wait(go, 1)

    @pl.when(w2 == 0)
    def _():
        pl.semaphore_wait(entered, 1)
        for hd in range(halves):
            cross(k, hd, k).start()
        pl.semaphore_wait(barrier, len(beside))
        for p in beside:
            signal(round_sem, p)
        pl.semaphore_wait(round_sem, len(beside))
        signal(go, across)

    for hd in range(halves):
        cross(1 - k, hd, k).start()
    for p in beside:
        forward(p, me).start()
    fetch = [pltpu.make_async_copy(order_hbm, order_ref, load.at[0]),
             pltpu.make_async_copy(bank_hbm, bank_ref, load.at[1])]
    stay = pltpu.make_async_copy(piece(x_ref, me), held(buf, me), own.at[0])
    for copy in fetch + [stay]:
        copy.start()
    for copy in fetch:
        copy.wait()

    gates = [bank_ref[order_ref[j]] for j in range(4)]
    first = embed(gates[0][0], gates[0][1])
    third = embed(gates[2][0], gates[2][1])
    for i, part in enumerate(split(dot(first, third, ((0,), (1,))))):
        lanes_gate[i] = part
    real, imag = 0.0, 0.0
    for high in range(2):
        spread = spread_rows(groups, mid, gate_rows, high)
        real += dot_t(dot(spread, gates[3][0]), spread)
        imag += dot_t(dot(spread, gates[3][1]), spread)
    zero = jnp.zeros((gate_rows, gate_rows), jnp.float32)
    parts = []
    for part in range(2):
        g = gates[1][part]
        parts.append(jnp.concatenate([
            jnp.concatenate([g, zero], axis=1), jnp.concatenate([zero, g], axis=1)], axis=0))
    for i, part in enumerate(split(dot(embed(real, imag), jnp.concatenate(parts, axis=0)))):
        rows_gate[i] = part

    keep = []
    for flip in range(2):
        ks = k if flip == 0 else 1 - k
        for hd in range(halves):
            cross(ks, hd, ks).wait_recv()
        for dest in plane[1:]:
            relay(*dest, ks, h, w0).start()
        keep.append(pltpu.make_async_copy(
            landed.at[ks, h, :, w0], held(buf, (h * 2 + ks, other, w0)), own.at[1 + flip]))
        keep[-1].start()

    for p in beside:
        forward(p, p).wait_recv()
    for flip in range(2):
        ks = k if flip == 0 else 1 - k
        for src in plane[1:]:
            relay(*src, ks, *src).wait_recv()
    for copy in [stay] + keep:
        copy.wait()

    flat_in = buf.reshape(rows * sub, buf.shape[-1])
    flat_out = obuf.reshape(rows * sub, buf.shape[-1])
    for q in range(sub // 2):
        re = flat_in[pl.ds(2 * q, rows, sub), :]
        im = flat_in[pl.ds(2 * q + 1, rows, sub), :]
        mixed = dot3(split(jnp.concatenate([re, im], axis=1)), lanes_gate)
        done = dot3(rows_gate, split(mixed))
        flat_out[pl.ds(2 * q, rows, sub), :] = done[:rows, :gate_rows] - done[rows:, gate_rows:]
        flat_out[pl.ds(2 * q + 1, rows, sub), :] = done[:rows, gate_rows:] + done[rows:, :gate_rows]

    local = []
    for kd in (1, 0):
        for dest in plane[1:]:
            gather(*dest, kd, h, w0).start()
        local.append(pltpu.make_async_copy(
            held(obuf, (h * 2 + kd, other, w0)), stage.at[kd, h, :, w0], own.at[1 + kd]))
        local[-1].start()
    for p in beside:
        back(p, me).start()
    stay = pltpu.make_async_copy(held(obuf, me), piece(out_ref, me), own.at[0])
    stay.start()

    for kd in (1, 0):
        for src in plane[1:]:
            gather(*src, kd, *src).wait_recv()
        local[1 - kd].wait()
        for hs in range(halves):
            home(kd, hs, k, w2).start()

    for p in beside:
        back(p, p).wait_recv()
    stay.wait()
    for ks in range(2):
        for hs in range(halves):
            home(ks, hs, ks, other).wait_recv()
    for kd in range(2):
        for hd in range(halves):
            cross(kd, hd, k).wait_send()
            home(kd, hd, k, w2).wait_send()
        for dest in plane[1:]:
            relay(*dest, kd, h, w0).wait_send()
            gather(*dest, kd, h, w0).wait_send()
    for p in beside:
        forward(p, me).wait_send()
        back(p, me).wait_send()


def per_device(groups, wa_count, state, gate_bank, pass_order):
    lanes = gate_bank.shape[2]
    mid = lanes // (2 * groups)
    size = state.shape[1]
    sub = 2 * size // (lanes * 4 * groups * mid)
    shape = (groups // 2, 2, 2, mid, 2, sub, lanes)
    x = state.reshape(2, size // lanes, lanes).transpose(1, 0, 2).reshape(shape)
    slots = 4 * groups
    dma = pltpu.SemaphoreType.DMA
    out = pl.pallas_call(
        functools.partial(kernel, groups, wa_count, mid, sub),
        out_shape=pltpu.VMEM(shape, jnp.float32),
        in_specs=[pl.BlockSpec(memory_space=pl.ANY)] * 3,
        out_specs=pl.BlockSpec(memory_space=pltpu.VMEM),
        scratch_shapes=[
            pltpu.SMEM(pass_order.shape, jnp.int32),
            pltpu.VMEM(gate_bank.shape, jnp.float32),
            pltpu.VMEM((2, 2 * lanes, 2 * lanes), jnp.bfloat16),
            pltpu.VMEM((2, 4 * lanes, 2 * lanes), jnp.bfloat16),
            pltpu.VMEM((2 * lanes, sub, lanes), jnp.float32),
            pltpu.VMEM((2 * lanes, sub, lanes), jnp.float32),
            pltpu.VMEM((2, groups // 2, mid, 2, sub, lanes), jnp.float32),
            pltpu.VMEM((2, groups // 2, mid, 2, sub, lanes), jnp.float32),
            dma((2, groups // 2)), dma((2, groups // 2)),
            dma((2, groups // 2)), dma((2, groups // 2)),
            dma((slots,)), dma((slots,)), dma((slots,)), dma((slots,)),
            dma((3,)), dma((2,)),
            pltpu.SemaphoreType.REGULAR, pltpu.SemaphoreType.REGULAR,
            pltpu.SemaphoreType.REGULAR,
        ],
        compiler_params=pltpu.CompilerParams(collective_id=0, has_side_effects=True),
    )(pass_order, gate_bank, x)
    return out.reshape(size // lanes, 2, lanes).transpose(1, 0, 2).reshape(2, size)


def solution(mesh):
    in_specs = (P(None, ("pb", "wa")), P(), P())
    out_specs = P(None, ("pb", "wa"))
    return jax.shard_map(
        functools.partial(per_device, mesh.shape["pb"], mesh.shape["wa"]),
        mesh=mesh, in_specs=in_specs, out_specs=out_specs, check_vma=False,
    )
```

```python
import functools

import jax
import jax.numpy as jnp
from jax import lax
from jax.experimental import pallas as pl
from jax.experimental.pallas import tpu as pltpu
from jax.sharding import PartitionSpec as P

MESH = pl.DeviceIdType.MESH
HIGH = lax.Precision.HIGHEST


def dot(a, b, contract=((1,), (0,)), precision=HIGH):
    return lax.dot_general(
        a, b, (contract, ((), ())), precision=precision, preferred_element_type=jnp.float32
    )


def dot_t(a, b):
    return dot(a, b, ((1,), (1,)))


def embed(real, imag):
    upper = jnp.concatenate([real, -imag], axis=1)
    lower = jnp.concatenate([imag, real], axis=1)
    return jnp.concatenate([upper, lower], axis=0)


def split(values):
    high = values.astype(jnp.bfloat16)
    return high, (values - high.astype(jnp.float32)).astype(jnp.bfloat16)


def dot3(a, b):
    def term(i, j):
        return dot(a[i], b[j], precision=None)

    return term(0, 0) + (term(0, 1) + term(1, 0))


def spread_rows(groups, mid, gate_rows, high):
    slot = lax.broadcasted_iota(jnp.int32, (2 * gate_rows, gate_rows), 0)
    row = lax.broadcasted_iota(jnp.int32, (2 * gate_rows, gate_rows), 1)
    a = row // (2 * mid)
    w0 = (row // mid) % 2
    m = row % mid
    return jnp.where(slot == ((w0 * groups + a) * 2 + high) * mid + m, 1.0, 0.0).astype(jnp.float32)


def kernel(groups, wa_count, mid, sub, order_hbm, bank_hbm, x_ref, out_ref, order_ref, bank_ref,
           lanes_gate, rows_gate, buf, obuf, landed, stage, early, zfs, zfr, zbs, zbr, fs, fr, bs, br,
           own, load, entered, round_sem, go):
    gate_rows = bank_ref.shape[2]
    rows = 2 * gate_rows
    halves = groups // 2
    a = lax.axis_index("pb")
    w = lax.axis_index("wa")
    half = wa_count // 2
    w2 = w // half
    w0 = w % 2
    wm = w - w2 * half - w0
    other = 1 - w2
    h = a // 2
    k = a % 2
    me = (a, w2, w0)

    def device(p):
        return (p[0], p[1] * half + wm + p[2])

    def slot(p):
        return (p[2] * groups + p[0]) * 2 + p[1]

    def held(ref, p):
        return ref.at[pl.ds(slot(p) * mid, mid)]

    def piece(ref, p):
        return ref.at[p[0] // 2, p[0] % 2, p[1], :, p[2]]

    beside = [((a + da) % groups, w2, (w0 + dw0) % 2)
              for da in range(groups) for dw0 in range(2)][1:]
    plane = [((h + dh) % halves, (w0 + dw0) % 2) for dh in range(halves) for dw0 in range(2)]
    across = (a, other, w0)
    mine_last = [(h + 1 + dh) % halves for dh in range(halves)]
    mine_first = [(h + dh) % halves for dh in range(halves)]
    outer = (2 * wm >= half) & (w2 == 1)

    def by_place(step):
        pl.when(outer)(lambda: step(True))
        pl.when(jnp.logical_not(outer))(lambda: step(False))


    def remote(src, dst, send, recv, p):
        return pltpu.make_async_remote_copy(
            src_ref=src, dst_ref=dst, send_sem=send, recv_sem=recv,
            device_id=device(p), device_id_type=MESH)

    def cross(kd, hd, ks):
        return remote(x_ref.at[hd, kd, other], landed.at[ks, hd],
                      zfs.at[kd, hd], zfr.at[ks, hd], (h * 2 + kd, other, w0))

    def forward(p, src):
        return remote(piece(x_ref, p), held(buf, src), fs.at[slot(p)], fr.at[slot(src)], p)

    def relay(hd, xd, ks, src_h, src_x):
        src = (src_h * 2 + ks, other, src_x)
        return remote(landed.at[ks, hd, :, xd], held(buf, src),
                      fs.at[slot((hd * 2 + ks, other, xd))], fr.at[slot(src)],
                      (hd * 2 + k, w2, xd))

    def back(p, src):
        return remote(held(obuf, p), piece(out_ref, src), bs.at[slot(p)], br.at[slot(src)], p)

    def gather(hd, xd, kd, src_h, src_x):
        dst = (hd * 2 + kd, other, xd)
        return remote(held(obuf, dst), stage.at[kd, src_h, :, src_x],
                      bs.at[slot(dst)], br.at[slot((src_h * 2 + kd, other, src_x))],
                      (hd * 2 + k, w2, xd))

    def home(kd, hs, ks, side):
        return remote(stage.at[kd, hs], out_ref.at[hs, ks, side],
                      zbs.at[kd, hs], zbr.at[ks, hs], (h * 2 + kd, other, w0))

    def signal(sem, p):
        pl.semaphore_signal(sem, inc=1, device_id=device(p), device_id_type=MESH)

    barrier = pltpu.get_barrier_semaphore()

    ahead = pltpu.make_async_copy(x_ref.at[mine_last[0], k, other], early, own.at[3])

    @pl.when(w2 == 0)
    def _():
        signal(barrier, across)
        ahead.start()
        for p in beside:
            signal(barrier, p)

    @pl.when(w2 == 1)
    def _():
        pl.semaphore_wait(barrier, 1)
        signal(entered, across)
        for hd in mine_last:
            cross(k, hd, k).start()
        pl.semaphore_wait(go, 1)

    @pl.when(w2 == 0)
    def _():
        ahead.wait()
        pl.semaphore_wait(entered, 1)
        remote(early, landed.at[k, mine_last[0]], zfs.at[k, mine_last[0]],
               zfr.at[k, mine_last[0]], across).start()
        for hd in mine_last[1:]:
            cross(k, hd, k).start()
        pl.semaphore_wait(barrier, len(beside))
        for p in beside:
            signal(round_sem, p)
        pl.semaphore_wait(round_sem, len(beside))
        signal(go, across)

    for hd in mine_last:
        cross(1 - k, hd, k).start()
    for p in beside:
        forward(p, me).start()
    fetch = [pltpu.make_async_copy(order_hbm, order_ref, load.at[0]),
             pltpu.make_async_copy(bank_hbm, bank_ref, load.at[1])]
    stay = pltpu.make_async_copy(piece(x_ref, me), held(buf, me), own.at[0])
    for copy in fetch + [stay]:
        copy.start()
    for copy in fetch:
        copy.wait()

    gates = [bank_ref[order_ref[j]] for j in range(4)]
    first = embed(gates[0][0], gates[0][1])
    third = embed(gates[2][0], gates[2][1])
    for i, part in enumerate(split(dot(first, third, ((0,), (1,))))):
        lanes_gate[i] = part
    real, imag = 0.0, 0.0
    for high in range(2):
        spread = spread_rows(groups, mid, gate_rows, high)
        real += dot_t(dot(spread, gates[3][0]), spread)
        imag += dot_t(dot(spread, gates[3][1]), spread)
    zero = jnp.zeros((gate_rows, gate_rows), jnp.float32)
    parts = []
    for part in range(2):
        g = gates[1][part]
        parts.append(jnp.concatenate([
            jnp.concatenate([g, zero], axis=1), jnp.concatenate([zero, g], axis=1)], axis=0))
    for i, part in enumerate(split(dot(embed(real, imag), jnp.concatenate(parts, axis=0)))):
        rows_gate[i] = part

    def keep(ks):
        return pltpu.make_async_copy(
            landed.at[ks, h, :, w0], held(buf, (h * 2 + ks, other, w0)), own.at[1 + ks])

    def hand_on(far):
        for ks in (k, 1 - k):
            if far:
                for hd in range(halves):
                    cross(ks, hd, ks).wait_recv()
                for dest in plane[1:]:
                    relay(*dest, ks, h, w0).start()
            else:
                for j, hd in enumerate(mine_last):
                    cross(ks, hd, ks).wait_recv()
                    for dw0 in (1, 0) if j + 1 < halves else (1,):
                        relay(hd, (w0 + dw0) % 2, ks, h, w0).start()
            keep(ks).start()

    by_place(hand_on)

    for p in beside:
        forward(p, p).wait_recv()
    for flip in range(2):
        ks = k if flip == 0 else 1 - k
        for src in plane[1:]:
            relay(*src, ks, *src).wait_recv()
    for copy in (stay, keep(0), keep(1)):
        copy.wait()

    flat_in = buf.reshape(rows * sub, buf.shape[-1])
    flat_out = obuf.reshape(rows * sub, buf.shape[-1])
    for q in range(sub // 2):
        re = flat_in[pl.ds(2 * q, rows, sub), :]
        im = flat_in[pl.ds(2 * q + 1, rows, sub), :]
        mixed = dot3(split(jnp.concatenate([re, im], axis=1)), lanes_gate)
        done = dot3(rows_gate, split(mixed))
        flat_out[pl.ds(2 * q, rows, sub), :] = done[:rows, :gate_rows] - done[rows:, gate_rows:]
        flat_out[pl.ds(2 * q + 1, rows, sub), :] = done[:rows, gate_rows:] + done[rows:, :gate_rows]

    local = []
    for kd in (1, 0):
        for dest in plane[1:]:
            gather(*dest, kd, h, w0).start()
        local.append(pltpu.make_async_copy(
            held(obuf, (h * 2 + kd, other, w0)), stage.at[kd, h, :, w0], own.at[1 + kd]))
        local[-1].start()
    for p in beside:
        back(p, me).start()
    stay = pltpu.make_async_copy(held(obuf, me), piece(out_ref, me), own.at[0])
    stay.start()

    def send_home(far):
        for kd in (1, 0):
            local[1 - kd].wait()
            if far:
                for src in plane[1:]:
                    gather(*src, kd, *src).wait_recv()
                for hs in range(halves):
                    home(kd, hs, k, w2).start()
            else:
                for j, hs in enumerate(mine_first):
                    for dw0 in (1, 0) if j else (1,):
                        src = (hs, (w0 + dw0) % 2)
                        gather(*src, kd, *src).wait_recv()
                    home(kd, hs, k, w2).start()

    by_place(send_home)

    for p in beside:
        back(p, p).wait_recv()
    stay.wait()
    for ks in range(2):
        for hs in range(halves):
            home(ks, hs, ks, other).wait_recv()
    for kd in range(2):
        for hd in range(halves):
            cross(kd, hd, k).wait_send()
            home(kd, hd, k, w2).wait_send()
        for dest in plane[1:]:
            relay(*dest, kd, h, w0).wait_send()
            gather(*dest, kd, h, w0).wait_send()
    for p in beside:
        forward(p, me).wait_send()
        back(p, me).wait_send()


def per_device(groups, wa_count, state, gate_bank, pass_order):
    lanes = gate_bank.shape[2]
    mid = lanes // (2 * groups)
    size = state.shape[1]
    sub = 2 * size // (lanes * 4 * groups * mid)
    shape = (groups // 2, 2, 2, mid, 2, sub, lanes)
    x = state.reshape(2, size // lanes, lanes).transpose(1, 0, 2).reshape(shape)
    slots = 4 * groups
    dma = pltpu.SemaphoreType.DMA
    out = pl.pallas_call(
        functools.partial(kernel, groups, wa_count, mid, sub),
        out_shape=pltpu.VMEM(shape, jnp.float32),
        in_specs=[pl.BlockSpec(memory_space=pl.ANY)] * 3,
        out_specs=pl.BlockSpec(memory_space=pltpu.VMEM),
        scratch_shapes=[
            pltpu.SMEM(pass_order.shape, jnp.int32),
            pltpu.VMEM(gate_bank.shape, jnp.float32),
            pltpu.VMEM((2, 2 * lanes, 2 * lanes), jnp.bfloat16),
            pltpu.VMEM((2, 4 * lanes, 2 * lanes), jnp.bfloat16),
            pltpu.VMEM((2 * lanes, sub, lanes), jnp.float32),
            pltpu.VMEM((2 * lanes, sub, lanes), jnp.float32),
            pltpu.VMEM((2, groups // 2, mid, 2, sub, lanes), jnp.float32),
            pltpu.VMEM((2, groups // 2, mid, 2, sub, lanes), jnp.float32),
            pltpu.VMEM((mid, 2, sub, lanes), jnp.float32),
            dma((2, groups // 2)), dma((2, groups // 2)),
            dma((2, groups // 2)), dma((2, groups // 2)),
            dma((slots,)), dma((slots,)), dma((slots,)), dma((slots,)),
            dma((4,)), dma((2,)),
            pltpu.SemaphoreType.REGULAR, pltpu.SemaphoreType.REGULAR,
            pltpu.SemaphoreType.REGULAR,
        ],
        compiler_params=pltpu.CompilerParams(collective_id=0, has_side_effects=True),
    )(pass_order, gate_bank, x)
    return out.reshape(size // lanes, 2, lanes).transpose(1, 0, 2).reshape(2, size)


def solution(mesh):
    in_specs = (P(None, ("pb", "wa")), P(), P())
    out_specs = P(None, ("pb", "wa"))
    return jax.shard_map(
        functools.partial(per_device, mesh.shape["pb"], mesh.shape["wa"]),
        mesh=mesh, in_specs=in_specs, out_specs=out_specs, check_vma=False,
    )
```

```python
import functools

import jax
import jax.numpy as jnp
from jax import lax
from jax.experimental import pallas as pl
from jax.experimental.pallas import tpu as pltpu
from jax.sharding import PartitionSpec as P

MESH = pl.DeviceIdType.MESH
HIGH = lax.Precision.HIGHEST


def dot(a, b, contract=((1,), (0,)), precision=HIGH):
    return lax.dot_general(
        a, b, (contract, ((), ())), precision=precision, preferred_element_type=jnp.float32
    )


def dot_t(a, b):
    return dot(a, b, ((1,), (1,)))


def embed(real, imag):
    upper = jnp.concatenate([real, -imag], axis=1)
    lower = jnp.concatenate([imag, real], axis=1)
    return jnp.concatenate([upper, lower], axis=0)


def split(values):
    parts = []
    for _ in range(3):
        parts.append(values.astype(jnp.bfloat16))
        values = values - parts[-1].astype(jnp.float32)
    return parts


def dot_parts(a, b):
    def terms(order):
        return sum(dot(a[i], b[order - i], precision=None) for i in range(order + 1))

    return terms(0) + (terms(1) + terms(2))


def spread_rows(groups, mid, gate_rows, high):
    slot = lax.broadcasted_iota(jnp.int32, (2 * gate_rows, gate_rows), 0)
    row = lax.broadcasted_iota(jnp.int32, (2 * gate_rows, gate_rows), 1)
    a = row // (2 * mid)
    w0 = (row // mid) % 2
    m = row % mid
    return jnp.where(slot == ((w0 * groups + a) * 2 + high) * mid + m, 1.0, 0.0).astype(jnp.float32)


def kernel(groups, wa_count, mid, sub, order_hbm, bank_hbm, x_ref, out_ref, order_ref, bank_ref,
           lanes_gate, rows_gate, buf, obuf, landed, stage, early, zfs, zfr, zbs, zbr, fs, fr, bs, br,
           own, load, entered, round_sem, go):
    gate_rows = bank_ref.shape[2]
    rows = 2 * gate_rows
    halves = groups // 2
    a = lax.axis_index("pb")
    w = lax.axis_index("wa")
    half = wa_count // 2
    w2 = w // half
    w0 = w % 2
    wm = w - w2 * half - w0
    other = 1 - w2
    h = a // 2
    k = a % 2
    me = (a, w2, w0)

    def device(p):
        return (p[0], p[1] * half + wm + p[2])

    def slot(p):
        return (p[2] * groups + p[0]) * 2 + p[1]

    def held(ref, p):
        return ref.at[pl.ds(slot(p) * mid, mid)]

    def piece(ref, p):
        return ref.at[p[0] // 2, p[0] % 2, p[1], :, p[2]]

    beside = [((a + da) % groups, w2, (w0 + dw0) % 2)
              for da in range(groups) for dw0 in range(2)][1:]
    plane = [((h + dh) % halves, (w0 + dw0) % 2) for dh in range(halves) for dw0 in range(2)]
    across = (a, other, w0)
    mine_last = [(h + 1 + dh) % halves for dh in range(halves)]
    mine_first = [(h + dh) % halves for dh in range(halves)]
    outer = (2 * wm >= half) & (w2 == 1)

    def by_place(batch, step):
        pl.when(batch)(lambda: step(True))
        pl.when(jnp.logical_not(batch))(lambda: step(False))


    def remote(src, dst, send, recv, p):
        return pltpu.make_async_remote_copy(
            src_ref=src, dst_ref=dst, send_sem=send, recv_sem=recv,
            device_id=device(p), device_id_type=MESH)

    def cross(kd, hd, ks):
        return remote(x_ref.at[hd, kd, other], landed.at[ks, hd],
                      zfs.at[kd, hd], zfr.at[ks, hd], (h * 2 + kd, other, w0))

    def forward(p, src):
        return remote(piece(x_ref, p), held(buf, src), fs.at[slot(p)], fr.at[slot(src)], p)

    def relay(hd, xd, ks, src_h, src_x):
        src = (src_h * 2 + ks, other, src_x)
        return remote(landed.at[ks, hd, :, xd], held(buf, src),
                      fs.at[slot((hd * 2 + ks, other, xd))], fr.at[slot(src)],
                      (hd * 2 + k, w2, xd))

    def back(p, src):
        return remote(held(obuf, p), piece(out_ref, src), bs.at[slot(p)], br.at[slot(src)], p)

    def gather(hd, xd, kd, src_h, src_x):
        dst = (hd * 2 + kd, other, xd)
        return remote(held(obuf, dst), stage.at[kd, src_h, :, src_x],
                      bs.at[slot(dst)], br.at[slot((src_h * 2 + kd, other, src_x))],
                      (hd * 2 + k, w2, xd))

    def home(kd, hs, ks, side):
        return remote(stage.at[kd, hs], out_ref.at[hs, ks, side],
                      zbs.at[kd, hs], zbr.at[ks, hs], (h * 2 + kd, other, w0))

    def signal(sem, p):
        pl.semaphore_signal(sem, inc=1, device_id=device(p), device_id_type=MESH)

    barrier = pltpu.get_barrier_semaphore()

    ahead = pltpu.make_async_copy(x_ref.at[mine_last[0], k, other], early, own.at[3])

    @pl.when(w2 == 0)
    def _():
        signal(barrier, across)
        ahead.start()
        for p in beside:
            signal(barrier, p)

    @pl.when(w2 == 1)
    def _():
        pl.semaphore_wait(barrier, 1)
        signal(entered, across)
        for hd in mine_last:
            cross(k, hd, k).start()
        pl.semaphore_wait(go, 1)

    @pl.when(w2 == 0)
    def _():
        ahead.wait()
        pl.semaphore_wait(entered, 1)
        remote(early, landed.at[k, mine_last[0]], zfs.at[k, mine_last[0]],
               zfr.at[k, mine_last[0]], across).start()
        for hd in mine_last[1:]:
            cross(k, hd, k).start()
        pl.semaphore_wait(barrier, len(beside))
        for p in beside:
            signal(round_sem, p)
        pl.semaphore_wait(round_sem, len(beside))
        signal(go, across)

    for hd in mine_last:
        cross(1 - k, hd, k).start()
    for p in beside:
        forward(p, me).start()
    fetch = [pltpu.make_async_copy(order_hbm, order_ref, load.at[0]),
             pltpu.make_async_copy(bank_hbm, bank_ref, load.at[1])]
    stay = pltpu.make_async_copy(piece(x_ref, me), held(buf, me), own.at[0])
    for copy in fetch + [stay]:
        copy.start()
    for copy in fetch:
        copy.wait()

    gates = [bank_ref[order_ref[j]] for j in range(4)]
    first = embed(gates[0][0], gates[0][1])
    third = embed(gates[2][0], gates[2][1])
    for i, part in enumerate(split(dot(first, third, ((0,), (1,))))):
        lanes_gate[i] = part
    real, imag = 0.0, 0.0
    for high in range(2):
        spread = spread_rows(groups, mid, gate_rows, high)
        real += dot_t(dot(spread, gates[3][0]), spread)
        imag += dot_t(dot(spread, gates[3][1]), spread)
    zero = jnp.zeros((gate_rows, gate_rows), jnp.float32)
    parts = []
    for part in range(2):
        g = gates[1][part]
        parts.append(jnp.concatenate([
            jnp.concatenate([g, zero], axis=1), jnp.concatenate([zero, g], axis=1)], axis=0))
    for i, part in enumerate(split(dot(embed(real, imag), jnp.concatenate(parts, axis=0)))):
        rows_gate[i] = part

    def keep(ks):
        return pltpu.make_async_copy(
            landed.at[ks, h, :, w0], held(buf, (h * 2 + ks, other, w0)), own.at[1 + ks])

    def hand_on(far):
        for ks in (k, 1 - k):
            if far:
                for hd in range(halves):
                    cross(ks, hd, ks).wait_recv()
                for dest in plane[1:]:
                    relay(*dest, ks, h, w0).start()
            else:
                for j, hd in enumerate(mine_last):
                    cross(ks, hd, ks).wait_recv()
                    for dw0 in (1, 0) if j + 1 < halves else (1,):
                        relay(hd, (w0 + dw0) % 2, ks, h, w0).start()
            keep(ks).start()

    by_place(outer & (k == 1), hand_on)

    for p in beside:
        forward(p, p).wait_recv()
    for flip in range(2):
        ks = k if flip == 0 else 1 - k
        for src in plane[1:]:
            relay(*src, ks, *src).wait_recv()
    for copy in (stay, keep(0), keep(1)):
        copy.wait()

    flat_in = buf.reshape(rows * sub, buf.shape[-1])
    flat_out = obuf.reshape(rows * sub, buf.shape[-1])
    for q in range(sub // 2):
        re = flat_in[pl.ds(2 * q, rows, sub), :]
        im = flat_in[pl.ds(2 * q + 1, rows, sub), :]
        mixed = dot_parts(split(jnp.concatenate([re, im], axis=1)), lanes_gate)
        done = dot_parts(rows_gate, split(mixed))
        flat_out[pl.ds(2 * q, rows, sub), :] = done[:rows, :gate_rows] - done[rows:, gate_rows:]
        flat_out[pl.ds(2 * q + 1, rows, sub), :] = done[:rows, gate_rows:] + done[rows:, :gate_rows]

    local = []
    for kd in (1, 0):
        for dest in plane[1:]:
            gather(*dest, kd, h, w0).start()
        local.append(pltpu.make_async_copy(
            held(obuf, (h * 2 + kd, other, w0)), stage.at[kd, h, :, w0], own.at[1 + kd]))
        local[-1].start()
    for p in beside:
        back(p, me).start()
    stay = pltpu.make_async_copy(held(obuf, me), piece(out_ref, me), own.at[0])
    stay.start()

    def send_home(far):
        for kd in (1, 0):
            local[1 - kd].wait()
            if far:
                for src in plane[1:]:
                    gather(*src, kd, *src).wait_recv()
                for hs in range(halves):
                    home(kd, hs, k, w2).start()
            else:
                for j, hs in enumerate(mine_first):
                    for dw0 in (1, 0) if j else (1,):
                        src = (hs, (w0 + dw0) % 2)
                        gather(*src, kd, *src).wait_recv()
                    home(kd, hs, k, w2).start()

    by_place(outer & (k == 0), send_home)

    for p in beside:
        back(p, p).wait_recv()
    stay.wait()
    for ks in range(2):
        for hs in range(halves):
            home(ks, hs, ks, other).wait_recv()
    for kd in range(2):
        for hd in range(halves):
            cross(kd, hd, k).wait_send()
            home(kd, hd, k, w2).wait_send()
        for dest in plane[1:]:
            relay(*dest, kd, h, w0).wait_send()
            gather(*dest, kd, h, w0).wait_send()
    for p in beside:
        forward(p, me).wait_send()
        back(p, me).wait_send()


def per_device(groups, wa_count, state, gate_bank, pass_order):
    lanes = gate_bank.shape[2]
    mid = lanes // (2 * groups)
    size = state.shape[1]
    sub = 2 * size // (lanes * 4 * groups * mid)
    shape = (groups // 2, 2, 2, mid, 2, sub, lanes)
    x = state.reshape(2, size // lanes, lanes).transpose(1, 0, 2).reshape(shape)
    slots = 4 * groups
    dma = pltpu.SemaphoreType.DMA
    out = pl.pallas_call(
        functools.partial(kernel, groups, wa_count, mid, sub),
        out_shape=pltpu.VMEM(shape, jnp.float32),
        in_specs=[pl.BlockSpec(memory_space=pl.ANY)] * 3,
        out_specs=pl.BlockSpec(memory_space=pltpu.VMEM),
        scratch_shapes=[
            pltpu.SMEM(pass_order.shape, jnp.int32),
            pltpu.VMEM(gate_bank.shape, jnp.float32),
            pltpu.VMEM((3, 2 * lanes, 2 * lanes), jnp.bfloat16),
            pltpu.VMEM((3, 4 * lanes, 2 * lanes), jnp.bfloat16),
            pltpu.VMEM((2 * lanes, sub, lanes), jnp.float32),
            pltpu.VMEM((2 * lanes, sub, lanes), jnp.float32),
            pltpu.VMEM((2, groups // 2, mid, 2, sub, lanes), jnp.float32),
            pltpu.VMEM((2, groups // 2, mid, 2, sub, lanes), jnp.float32),
            pltpu.VMEM((mid, 2, sub, lanes), jnp.float32),
            dma((2, groups // 2)), dma((2, groups // 2)),
            dma((2, groups // 2)), dma((2, groups // 2)),
            dma((slots,)), dma((slots,)), dma((slots,)), dma((slots,)),
            dma((4,)), dma((2,)),
            pltpu.SemaphoreType.REGULAR, pltpu.SemaphoreType.REGULAR,
            pltpu.SemaphoreType.REGULAR,
        ],
        compiler_params=pltpu.CompilerParams(collective_id=0, has_side_effects=True),
    )(pass_order, gate_bank, x)
    return out.reshape(size // lanes, 2, lanes).transpose(1, 0, 2).reshape(2, size)


def solution(mesh):
    in_specs = (P(None, ("pb", "wa")), P(), P())
    out_specs = P(None, ("pb", "wa"))
    return jax.shard_map(
        functools.partial(per_device, mesh.shape["pb"], mesh.shape["wa"]),
        mesh=mesh, in_specs=in_specs, out_specs=out_specs, check_vma=False,
    )
```

```python
import functools

import jax
import jax.numpy as jnp
from jax import lax
from jax.experimental import pallas as pl
from jax.experimental.pallas import tpu as pltpu
from jax.sharding import PartitionSpec as P

MESH = pl.DeviceIdType.MESH
HIGH = lax.Precision.HIGHEST


def dot(a, b, contract=((1,), (0,)), precision=HIGH):
    return lax.dot_general(
        a, b, (contract, ((), ())), precision=precision, preferred_element_type=jnp.float32
    )


def dot_t(a, b):
    return dot(a, b, ((1,), (1,)))


def embed(real, imag):
    upper = jnp.concatenate([real, -imag], axis=1)
    lower = jnp.concatenate([imag, real], axis=1)
    return jnp.concatenate([upper, lower], axis=0)


def split(values):
    high = values.astype(jnp.bfloat16)
    return high, (values - high.astype(jnp.float32)).astype(jnp.bfloat16)


def dot3(a, b):
    def term(i, j):
        return dot(a[i], b[j], precision=None)

    return term(0, 0) + (term(0, 1) + term(1, 0))


def spread_rows(groups, mid, gate_rows, high):
    slot = lax.broadcasted_iota(jnp.int32, (2 * gate_rows, gate_rows), 0)
    row = lax.broadcasted_iota(jnp.int32, (2 * gate_rows, gate_rows), 1)
    a = row // (2 * mid)
    w0 = (row // mid) % 2
    m = row % mid
    return jnp.where(slot == ((w0 * groups + a) * 2 + high) * mid + m, 1.0, 0.0).astype(jnp.float32)


def kernel(groups, wa_count, mid, sub, order_hbm, bank_hbm, x_ref, out_ref, order_ref, bank_ref,
           lanes_gate, rows_gate, buf, obuf, landed, stage, early, extra, zfs, zfr, zbs, zbr, fs, fr, bs, br,
           own, load, lent, entered, round_sem, go):
    gate_rows = bank_ref.shape[2]
    rows = 2 * gate_rows
    halves = groups // 2
    a = lax.axis_index("pb")
    w = lax.axis_index("wa")
    half = wa_count // 2
    w2 = w // half
    w0 = w % 2
    wm = w - w2 * half - w0
    other = 1 - w2
    h = a // 2
    k = a % 2
    me = (a, w2, w0)

    def device(p):
        return (p[0], p[1] * half + wm + p[2])

    def slot(p):
        return (p[2] * groups + p[0]) * 2 + p[1]

    def held(ref, p):
        return ref.at[pl.ds(slot(p) * mid, mid)]

    def piece(ref, p):
        return ref.at[p[0] // 2, p[0] % 2, p[1], :, p[2]]

    beside = [((a + da) % groups, w2, (w0 + dw0) % 2)
              for da in range(groups) for dw0 in range(2)][1:]
    plane = [((h + dh) % halves, (w0 + dw0) % 2) for dh in range(halves) for dw0 in range(2)]
    across = (a, other, w0)
    mine_last = [(h + 1 + dh) % halves for dh in range(halves)]
    mine_first = [(h + dh) % halves for dh in range(halves)]
    outer = (2 * wm >= half) & (w2 == 1)

    def by_place(step):
        pl.when(outer)(lambda: step(True))
        pl.when(jnp.logical_not(outer))(lambda: step(False))


    def remote(src, dst, send, recv, p):
        return pltpu.make_async_remote_copy(
            src_ref=src, dst_ref=dst, send_sem=send, recv_sem=recv,
            device_id=device(p), device_id_type=MESH)

    def cross(kd, hd, ks):
        return remote(x_ref.at[hd, kd, other], landed.at[ks, hd],
                      zfs.at[kd, hd], zfr.at[ks, hd], (h * 2 + kd, other, w0))

    def forward(p, src):
        return remote(piece(x_ref, p), held(buf, src), fs.at[slot(p)], fr.at[slot(src)], p)

    def relay(hd, xd, ks, src_h, src_x):
        src = (src_h * 2 + ks, other, src_x)
        return remote(landed.at[ks, hd, :, xd], held(buf, src),
                      fs.at[slot((hd * 2 + ks, other, xd))], fr.at[slot(src)],
                      (hd * 2 + k, w2, xd))

    def back(p, src):
        return remote(held(obuf, p), piece(out_ref, src), bs.at[slot(p)], br.at[slot(src)], p)

    def gather(hd, xd, kd, src_h, src_x):
        dst = (hd * 2 + kd, other, xd)
        return remote(held(obuf, dst), stage.at[kd, src_h, :, src_x],
                      bs.at[slot(dst)], br.at[slot((src_h * 2 + kd, other, src_x))],
                      (hd * 2 + k, w2, xd))

    def home(kd, hs, ks, side):
        return remote(stage.at[kd, hs], out_ref.at[hs, ks, side],
                      zbs.at[kd, hs], zbr.at[ks, hs], (h * 2 + kd, other, w0))

    def portion(x, side):
        return remote(stage.at[0, h, :, x], out_ref.at[h, 0, side, :, x],
                      zbs.at[0, h], zbr.at[0, h], across)

    def lend():
        return remote(held(obuf, (h * 2, other, w0)), extra, lent.at[0], lent.at[1], (h * 2 + 1, w2, w0))

    def carry(side):
        return remote(extra, out_ref.at[h, 0, side, :, w0], lent.at[2], lent.at[3], (h * 2, other, w0))

    def signal(sem, p):
        pl.semaphore_signal(sem, inc=1, device_id=device(p), device_id_type=MESH)

    barrier = pltpu.get_barrier_semaphore()

    ahead = pltpu.make_async_copy(x_ref.at[mine_last[0], k, other], early, own.at[3])

    @pl.when(w2 == 0)
    def _():
        signal(barrier, across)
        ahead.start()
        for p in beside:
            signal(barrier, p)

    @pl.when(w2 == 1)
    def _():
        pl.semaphore_wait(barrier, 1)
        signal(entered, across)
        for hd in mine_last:
            cross(k, hd, k).start()
        pl.semaphore_wait(go, 1)

    @pl.when(w2 == 0)
    def _():
        ahead.wait()
        pl.semaphore_wait(entered, 1)
        remote(early, landed.at[k, mine_last[0]], zfs.at[k, mine_last[0]],
               zfr.at[k, mine_last[0]], across).start()
        for hd in mine_last[1:]:
            cross(k, hd, k).start()
        pl.semaphore_wait(barrier, len(beside))
        for p in beside:
            signal(round_sem, p)
        pl.semaphore_wait(round_sem, len(beside))
        signal(go, across)

    for hd in mine_last:
        cross(1 - k, hd, k).start()
    for p in beside:
        forward(p, me).start()
    fetch = [pltpu.make_async_copy(order_hbm, order_ref, load.at[0]),
             pltpu.make_async_copy(bank_hbm, bank_ref, load.at[1])]
    stay = pltpu.make_async_copy(piece(x_ref, me), held(buf, me), own.at[0])
    for copy in fetch + [stay]:
        copy.start()
    for copy in fetch:
        copy.wait()

    gates = [bank_ref[order_ref[j]] for j in range(4)]
    first = embed(gates[0][0], gates[0][1])
    third = embed(gates[2][0], gates[2][1])
    for i, part in enumerate(split(dot(first, third, ((0,), (1,))))):
        lanes_gate[i] = part
    real, imag = 0.0, 0.0
    for high in range(2):
        spread = spread_rows(groups, mid, gate_rows, high)
        real += dot_t(dot(spread, gates[3][0]), spread)
        imag += dot_t(dot(spread, gates[3][1]), spread)
    zero = jnp.zeros((gate_rows, gate_rows), jnp.float32)
    parts = []
    for part in range(2):
        g = gates[1][part]
        parts.append(jnp.concatenate([
            jnp.concatenate([g, zero], axis=1), jnp.concatenate([zero, g], axis=1)], axis=0))
    for i, part in enumerate(split(dot(embed(real, imag), jnp.concatenate(parts, axis=0)))):
        rows_gate[i] = part

    def keep(ks):
        return pltpu.make_async_copy(
            landed.at[ks, h, :, w0], held(buf, (h * 2 + ks, other, w0)), own.at[1 + ks])

    def hand_on(far):
        for ks in (k, 1 - k):
            if far:
                for hd in range(halves):
                    cross(ks, hd, ks).wait_recv()
                for dest in plane[1:]:
                    relay(*dest, ks, h, w0).start()
            else:
                for j, hd in enumerate(mine_last):
                    cross(ks, hd, ks).wait_recv()
                    for dw0 in (1, 0) if j + 1 < halves else (1,):
                        relay(hd, (w0 + dw0) % 2, ks, h, w0).start()
            keep(ks).start()

    by_place(hand_on)

    for p in beside:
        forward(p, p).wait_recv()
    for flip in range(2):
        ks = k if flip == 0 else 1 - k
        for src in plane[1:]:
            relay(*src, ks, *src).wait_recv()
    for copy in (stay, keep(0), keep(1)):
        copy.wait()

    flat_in = buf.reshape(rows * sub, buf.shape[-1])
    flat_out = obuf.reshape(rows * sub, buf.shape[-1])
    for q in range(sub // 2):
        re = flat_in[pl.ds(2 * q, rows, sub), :]
        im = flat_in[pl.ds(2 * q + 1, rows, sub), :]
        mixed = dot3(split(jnp.concatenate([re, im], axis=1)), lanes_gate)
        done = dot3(rows_gate, split(mixed))
        flat_out[pl.ds(2 * q, rows, sub), :] = done[:rows, :gate_rows] - done[rows:, gate_rows:]
        flat_out[pl.ds(2 * q + 1, rows, sub), :] = done[:rows, gate_rows:] + done[rows:, :gate_rows]

    local = []
    for kd in (1, 0):
        for dest in plane[1:]:
            gather(*dest, kd, h, w0).start()
        local.append(pltpu.make_async_copy(
            held(obuf, (h * 2 + kd, other, w0)), stage.at[kd, h, :, w0], own.at[1 + kd]))
        if kd == 1:
            local[-1].start()
        else:
            pl.when(k == 1)(local[-1].start)
            pl.when(k == 0)(lambda: lend().start())
    for p in beside:
        back(p, me).start()
    stay = pltpu.make_async_copy(held(obuf, me), piece(out_ref, me), own.at[0])
    stay.start()

    def send_home(far):
        for kd in (1, 0):
            if kd == 1:
                local[0].wait()
            else:
                pl.when(k == 1)(local[1].wait)
            for j, hs in enumerate(mine_first):
                for dh in range(halves) if far and j == 0 else () if far else (j,):
                    for dw0 in (1, 0) if dh else (1,):
                        src = (mine_first[dh], (w0 + dw0) % 2)
                        gather(*src, kd, *src).wait_recv()
                if kd == 1 or j:
                    home(kd, hs, k, w2).start()
                else:
                    @pl.when(k == 1)
                    def _():
                        home(0, h, 1, w2).start()
                        lend().wait_recv()
                        carry(w2).start()

                    @pl.when(k == 0)
                    def _():
                        portion(1 - w0, w2).start()

    by_place(send_home)

    for p in beside:
        back(p, p).wait_recv()
    stay.wait()
    for ks in range(2):
        for hs in mine_first:
            if ks == 0 and hs is mine_first[0]:
                @pl.when(k == 0)
                def _():
                    portion(1 - w0, other).wait_recv()
                    carry(other).wait_recv()

                @pl.when(k == 1)
                def _():
                    home(0, h, 0, other).wait_recv()
            else:
                home(ks, hs, ks, other).wait_recv()
    for kd in range(2):
        for hd in range(halves):
            cross(kd, hd, k).wait_send()
        for dest in plane[1:]:
            relay(*dest, kd, h, w0).wait_send()
            gather(*dest, kd, h, w0).wait_send()
        for hd in mine_first[1 - kd:]:
            home(kd, hd, k, w2).wait_send()

    @pl.when(k == 0)
    def _():
        portion(1 - w0, w2).wait_send()
        lend().wait_send()

    @pl.when(k == 1)
    def _():
        home(0, h, 1, w2).wait_send()
        carry(w2).wait_send()

    for p in beside:
        forward(p, me).wait_send()
        back(p, me).wait_send()


def per_device(groups, wa_count, state, gate_bank, pass_order):
    lanes = gate_bank.shape[2]
    mid = lanes // (2 * groups)
    size = state.shape[1]
    sub = 2 * size // (lanes * 4 * groups * mid)
    shape = (groups // 2, 2, 2, mid, 2, sub, lanes)
    x = state.reshape(2, size // lanes, lanes).transpose(1, 0, 2).reshape(shape)
    slots = 4 * groups
    dma = pltpu.SemaphoreType.DMA
    out = pl.pallas_call(
        functools.partial(kernel, groups, wa_count, mid, sub),
        out_shape=pltpu.VMEM(shape, jnp.float32),
        in_specs=[pl.BlockSpec(memory_space=pl.ANY)] * 3,
        out_specs=pl.BlockSpec(memory_space=pltpu.VMEM),
        scratch_shapes=[
            pltpu.SMEM(pass_order.shape, jnp.int32),
            pltpu.VMEM(gate_bank.shape, jnp.float32),
            pltpu.VMEM((2, 2 * lanes, 2 * lanes), jnp.bfloat16),
            pltpu.VMEM((2, 4 * lanes, 2 * lanes), jnp.bfloat16),
            pltpu.VMEM((2 * lanes, sub, lanes), jnp.float32),
            pltpu.VMEM((2 * lanes, sub, lanes), jnp.float32),
            pltpu.VMEM((2, groups // 2, mid, 2, sub, lanes), jnp.float32),
            pltpu.VMEM((2, groups // 2, mid, 2, sub, lanes), jnp.float32),
            pltpu.VMEM((mid, 2, sub, lanes), jnp.float32),
            pltpu.VMEM((mid, sub, lanes), jnp.float32),
            dma((2, groups // 2)), dma((2, groups // 2)),
            dma((2, groups // 2)), dma((2, groups // 2)),
            dma((slots,)), dma((slots,)), dma((slots,)), dma((slots,)),
            dma((4,)), dma((2,)), dma((4,)),
            pltpu.SemaphoreType.REGULAR, pltpu.SemaphoreType.REGULAR,
            pltpu.SemaphoreType.REGULAR,
        ],
        compiler_params=pltpu.CompilerParams(collective_id=0, has_side_effects=True),
    )(pass_order, gate_bank, x)
    return out.reshape(size // lanes, 2, lanes).transpose(1, 0, 2).reshape(2, size)


def solution(mesh):
    in_specs = (P(None, ("pb", "wa")), P(), P())
    out_specs = P(None, ("pb", "wa"))
    return jax.shard_map(
        functools.partial(per_device, mesh.shape["pb"], mesh.shape["wa"]),
        mesh=mesh, in_specs=in_specs, out_specs=out_specs, check_vma=False,
    )
```

```python
import functools

import jax
import jax.numpy as jnp
from jax import lax
from jax.experimental import pallas as pl
from jax.experimental.pallas import tpu as pltpu
from jax.sharding import PartitionSpec as P

MESH = pl.DeviceIdType.MESH
HIGH = lax.Precision.HIGHEST


def dot(a, b, contract=((1,), (0,)), precision=HIGH):
    return lax.dot_general(
        a, b, (contract, ((), ())), precision=precision, preferred_element_type=jnp.float32
    )


def dot_t(a, b):
    return dot(a, b, ((1,), (1,)))


def embed(real, imag):
    upper = jnp.concatenate([real, -imag], axis=1)
    lower = jnp.concatenate([imag, real], axis=1)
    return jnp.concatenate([upper, lower], axis=0)


def split(values):
    high = values.astype(jnp.bfloat16)
    return high, (values - high.astype(jnp.float32)).astype(jnp.bfloat16)


def dot3(a, b):
    def term(i, j):
        return dot(a[i], b[j], precision=None)

    return term(0, 0) + (term(0, 1) + term(1, 0))


def spread_rows(groups, mid, gate_rows, high):
    slot = lax.broadcasted_iota(jnp.int32, (2 * gate_rows, gate_rows), 0)
    row = lax.broadcasted_iota(jnp.int32, (2 * gate_rows, gate_rows), 1)
    a = row // (2 * mid)
    w0 = (row // mid) % 2
    m = row % mid
    return jnp.where(slot == ((w0 * groups + a) * 2 + high) * mid + m, 1.0, 0.0).astype(jnp.float32)


def kernel(groups, wa_count, mid, sub, order_hbm, bank_hbm, x_ref, out_ref, order_ref, bank_ref,
           lanes_gate, rows_gate, buf, obuf, landed, stage, early, zfs, zfr, zbs, zbr, fs, fr, bs, br,
           own, load, entered, round_sem, go):
    gate_rows = bank_ref.shape[2]
    rows = 2 * gate_rows
    halves = groups // 2
    a = lax.axis_index("pb")
    w = lax.axis_index("wa")
    half = wa_count // 2
    w2 = w // half
    w0 = w % 2
    wm = w - w2 * half - w0
    other = 1 - w2
    h = a // 2
    k = a % 2
    me = (a, w2, w0)

    def device(p):
        return (p[0], p[1] * half + wm + p[2])

    def slot(p):
        return (p[2] * groups + p[0]) * 2 + p[1]

    def held(ref, p):
        return ref.at[pl.ds(slot(p) * mid, mid)]

    def piece(ref, p):
        return ref.at[p[0] // 2, p[0] % 2, p[1], :, p[2]]

    beside = [((a + da) % groups, w2, (w0 + dw0) % 2)
              for da in range(groups) for dw0 in range(2)][1:]
    plane = [((h + dh) % halves, (w0 + dw0) % 2) for dh in range(halves) for dw0 in range(2)]
    across = (a, other, w0)
    mine_last = [(h + 1 + dh) % halves for dh in range(halves)]
    mine_first = [(h + dh) % halves for dh in range(halves)]
    outer = (2 * wm >= half) & (w2 == 1)

    def by_place(step):
        pl.when(outer)(lambda: step(True))
        pl.when(jnp.logical_not(outer))(lambda: step(False))


    def remote(src, dst, send, recv, p):
        return pltpu.make_async_remote_copy(
            src_ref=src, dst_ref=dst, send_sem=send, recv_sem=recv,
            device_id=device(p), device_id_type=MESH)

    def cross(kd, hd, ks):
        return remote(x_ref.at[hd, kd, other], landed.at[ks, hd],
                      zfs.at[kd, hd], zfr.at[ks, hd], (h * 2 + kd, other, w0))

    def forward(p, src):
        return remote(piece(x_ref, p), held(buf, src), fs.at[slot(p)], fr.at[slot(src)], p)

    def relay(hd, xd, ks, src_h, src_x):
        src = (src_h * 2 + ks, other, src_x)
        return remote(landed.at[ks, hd, :, xd], held(buf, src),
                      fs.at[slot((hd * 2 + ks, other, xd))], fr.at[slot(src)],
                      (hd * 2 + k, w2, xd))

    def back(p, src):
        return remote(held(obuf, p), piece(out_ref, src), bs.at[slot(p)], br.at[slot(src)], p)

    def gather(hd, xd, kd, src_h, src_x):
        dst = (hd * 2 + kd, other, xd)
        return remote(held(obuf, dst), stage.at[kd, src_h, :, src_x],
                      bs.at[slot(dst)], br.at[slot((src_h * 2 + kd, other, src_x))],
                      (hd * 2 + k, w2, xd))

    def home(kd, hs, ks, side):
        return remote(stage.at[kd, hs], out_ref.at[hs, ks, side],
                      zbs.at[kd, hs], zbr.at[ks, hs], (h * 2 + kd, other, w0))

    def signal(sem, p):
        pl.semaphore_signal(sem, inc=1, device_id=device(p), device_id_type=MESH)

    barrier = pltpu.get_barrier_semaphore()

    ahead = pltpu.make_async_copy(x_ref.at[mine_last[0], k, other], early, own.at[3])

    @pl.when(w2 == 0)
    def _():
        signal(barrier, across)
        ahead.start()
        for p in beside:
            signal(barrier, p)

    @pl.when(w2 == 1)
    def _():
        pl.semaphore_wait(barrier, 1)
        signal(entered, across)
        for hd in mine_last:
            cross(k, hd, k).start()
        pl.semaphore_wait(go, 1)

    @pl.when(w2 == 0)
    def _():
        ahead.wait()
        pl.semaphore_wait(entered, 1)
        remote(early, landed.at[k, mine_last[0]], zfs.at[k, mine_last[0]],
               zfr.at[k, mine_last[0]], across).start()
        for hd in mine_last[1:]:
            cross(k, hd, k).start()
        pl.semaphore_wait(barrier, len(beside))
        for p in beside:
            signal(round_sem, p)
        pl.semaphore_wait(round_sem, len(beside))
        signal(go, across)

    for hd in mine_last:
        cross(1 - k, hd, k).start()
    for p in beside:
        forward(p, me).start()
    fetch = [pltpu.make_async_copy(order_hbm, order_ref, load.at[0]),
             pltpu.make_async_copy(bank_hbm, bank_ref, load.at[1])]
    stay = pltpu.make_async_copy(piece(x_ref, me), held(buf, me), own.at[0])
    for copy in fetch + [stay]:
        copy.start()
    for copy in fetch:
        copy.wait()

    gates = [bank_ref[order_ref[j]] for j in range(4)]
    first = embed(gates[0][0], gates[0][1])
    third = embed(gates[2][0], gates[2][1])
    for i, part in enumerate(split(dot(first, third, ((0,), (1,))))):
        lanes_gate[i] = part
    real, imag = 0.0, 0.0
    for high in range(2):
        spread = spread_rows(groups, mid, gate_rows, high)
        real += dot_t(dot(spread, gates[3][0]), spread)
        imag += dot_t(dot(spread, gates[3][1]), spread)
    zero = jnp.zeros((gate_rows, gate_rows), jnp.float32)
    parts = []
    for part in range(2):
        g = gates[1][part]
        parts.append(jnp.concatenate([
            jnp.concatenate([g, zero], axis=1), jnp.concatenate([zero, g], axis=1)], axis=0))
    for i, part in enumerate(split(dot(embed(real, imag), jnp.concatenate(parts, axis=0)))):
        rows_gate[i] = part

    def keep(ks):
        return pltpu.make_async_copy(
            landed.at[ks, h, :, w0], held(buf, (h * 2 + ks, other, w0)), own.at[1 + ks])

    def hand_on(far):
        for ks in (k, 1 - k):
            if far:
                for hd in range(halves):
                    cross(ks, hd, ks).wait_recv()
                for dest in plane[1:]:
                    relay(*dest, ks, h, w0).start()
            else:
                for j, hd in enumerate(mine_last):
                    cross(ks, hd, ks).wait_recv()
                    for dw0 in (1, 0) if j + 1 < halves else (1,):
                        relay(hd, (w0 + dw0) % 2, ks, h, w0).start()
            keep(ks).start()

    by_place(hand_on)

    for p in beside:
        forward(p, p).wait_recv()
    for flip in range(2):
        ks = k if flip == 0 else 1 - k
        for src in plane[1:]:
            relay(*src, ks, *src).wait_recv()
    for copy in (stay, keep(0), keep(1)):
        copy.wait()

    flat_in = buf.reshape(rows * sub, buf.shape[-1])
    flat_out = obuf.reshape(rows * sub, buf.shape[-1])
    for q in range(sub // 2):
        re = flat_in[pl.ds(2 * q, rows, sub), :]
        im = flat_in[pl.ds(2 * q + 1, rows, sub), :]
        mixed = dot3(split(jnp.concatenate([re, im], axis=1)), lanes_gate)
        done = dot3(rows_gate, split(mixed))
        flat_out[pl.ds(2 * q, rows, sub), :] = done[:rows, :gate_rows] - done[rows:, gate_rows:]
        flat_out[pl.ds(2 * q + 1, rows, sub), :] = done[:rows, gate_rows:] + done[rows:, :gate_rows]

    def local(kd):
        return pltpu.make_async_copy(
            held(obuf, (h * 2 + kd, other, w0)), stage.at[kd, h, :, w0], own.at[1 + kd])

    for kd in (other, w2):
        for dest in plane[1:]:
            gather(*dest, kd, h, w0).start()
        local(kd).start()
    for p in beside:
        back(p, me).start()
    stay = pltpu.make_async_copy(held(obuf, me), piece(out_ref, me), own.at[0])
    stay.start()

    def send_home(far):
        for kd in (other, w2):
            local(kd).wait()
            if far:
                for src in plane[1:]:
                    gather(*src, kd, *src).wait_recv()
                for hs in range(halves):
                    home(kd, hs, k, w2).start()
            else:
                for j, hs in enumerate(mine_first):
                    for dw0 in (1, 0) if j else (1,):
                        src = (hs, (w0 + dw0) % 2)
                        gather(*src, kd, *src).wait_recv()
                    home(kd, hs, k, w2).start()

    by_place(send_home)

    for p in beside:
        back(p, p).wait_recv()
    stay.wait()
    for ks in range(2):
        for hs in range(halves):
            home(ks, hs, ks, other).wait_recv()
    for kd in range(2):
        for hd in range(halves):
            cross(kd, hd, k).wait_send()
            home(kd, hd, k, w2).wait_send()
        for dest in plane[1:]:
            relay(*dest, kd, h, w0).wait_send()
            gather(*dest, kd, h, w0).wait_send()
    for p in beside:
        forward(p, me).wait_send()
        back(p, me).wait_send()


def per_device(groups, wa_count, state, gate_bank, pass_order):
    lanes = gate_bank.shape[2]
    mid = lanes // (2 * groups)
    size = state.shape[1]
    sub = 2 * size // (lanes * 4 * groups * mid)
    shape = (groups // 2, 2, 2, mid, 2, sub, lanes)
    x = state.reshape(2, size // lanes, lanes).transpose(1, 0, 2).reshape(shape)
    slots = 4 * groups
    dma = pltpu.SemaphoreType.DMA
    out = pl.pallas_call(
        functools.partial(kernel, groups, wa_count, mid, sub),
        out_shape=pltpu.VMEM(shape, jnp.float32),
        in_specs=[pl.BlockSpec(memory_space=pl.ANY)] * 3,
        out_specs=pl.BlockSpec(memory_space=pltpu.VMEM),
        scratch_shapes=[
            pltpu.SMEM(pass_order.shape, jnp.int32),
            pltpu.VMEM(gate_bank.shape, jnp.float32),
            pltpu.VMEM((2, 2 * lanes, 2 * lanes), jnp.bfloat16),
            pltpu.VMEM((2, 4 * lanes, 2 * lanes), jnp.bfloat16),
            pltpu.VMEM((2 * lanes, sub, lanes), jnp.float32),
            pltpu.VMEM((2 * lanes, sub, lanes), jnp.float32),
            pltpu.VMEM((2, groups // 2, mid, 2, sub, lanes), jnp.float32),
            pltpu.VMEM((2, groups // 2, mid, 2, sub, lanes), jnp.float32),
            pltpu.VMEM((mid, 2, sub, lanes), jnp.float32),
            dma((2, groups // 2)), dma((2, groups // 2)),
            dma((2, groups // 2)), dma((2, groups // 2)),
            dma((slots,)), dma((slots,)), dma((slots,)), dma((slots,)),
            dma((4,)), dma((2,)),
            pltpu.SemaphoreType.REGULAR, pltpu.SemaphoreType.REGULAR,
            pltpu.SemaphoreType.REGULAR,
        ],
        compiler_params=pltpu.CompilerParams(collective_id=0, has_side_effects=True),
    )(pass_order, gate_bank, x)
    return out.reshape(size // lanes, 2, lanes).transpose(1, 0, 2).reshape(2, size)


def solution(mesh):
    in_specs = (P(None, ("pb", "wa")), P(), P())
    out_specs = P(None, ("pb", "wa"))
    return jax.shard_map(
        functools.partial(per_device, mesh.shape["pb"], mesh.shape["wa"]),
        mesh=mesh, in_specs=in_specs, out_specs=out_specs, check_vma=False,
    )
```
